32 devices in a mesh: blk: 8 (over z, y), rep: 4 (over x, core).
Axes of the slice: x: 2, y: 2, z: 4, core: 2. Of those that a mesh axis runs over, the one named last changes fastest.
Arguments:
- features: bfloat16 [8192, 256], P(('blk', 'rep')), may hold values from -6 to 6
- tiles: bfloat16 [8, 64, 128, 128], P('blk', 'rep'), may hold values from -0.25 to 0.25
- tile_rows: int32 [8, 64], P('blk', 'rep'), may hold values from 0 to 7
- tile_cols: int32 [8, 64], P('blk', 'rep'), may hold values from 0 to 15
- counts: int32 [8, 4], P('blk', 'rep'), may hold values from 4 to 16
- weight: bfloat16 [256, 256], replicated, may hold values from -0.375 to 0.375
- bias: float32 [256], replicated, may hold values from -3 to 3
- cotangent: bfloat16 [8192, 256], P(('blk', 'rep')), may hold values from -6 to 6
Outputs:
- activations: bfloat16 [8192, 256], P(('blk', 'rep'))
- feature_grad: bfloat16 [8192, 256], P(('blk', 'rep'))
- weight_grad: float32 [256, 256], replicated
- bias_grad: float32 [256], replicated
The draws below stay inside these ranges and needn't reach their ends.
All inputs are finite; a program needn't handle non-finite values.
Results may differ from the reference program's by a relative error of at most 0.006.
Values may be sent and summed in bfloat16 or wider, within the bound.
A program may use at most 64 MiB of HBM per device.

```python
import jax
import jax.numpy as jnp
from jax import lax

FEAT = 256
TILE = 128
SLOTS = 16
TPD = 2
NODES = 8192
N_BLK = 8
N_REP = 4


def place_ends(result, own_key, smallest, top_value):
    shape = result.shape
    spot = [jax.random.randint(jax.random.fold_in(own_key, axis), (), 0, shape[axis]) for axis in range(len(shape))]
    result = result.at[tuple(spot)].set(smallest)
    longest = shape.index(max(shape))
    spot[longest] = (spot[longest] + 1) % shape[longest]
    return result.at[tuple(spot)].set(top_value)


def block_scale(stream_key, shape, shards, least, high):
    def one(axis_at, parts):
        heights = jax.random.uniform(jax.random.fold_in(jax.random.fold_in(stream_key, 6), axis_at), (parts,), jnp.float32, least / len(shards), high / len(shards))
        return jnp.repeat(jnp.exp(heights), shape[axis_at] // parts).reshape((-1,) + (1,) * (len(shape) - axis_at - 1))

    gain = one(*shards[0])
    for cut in shards[1:]:
        gain = gain * one(*cut)
    return gain


def normal_values(key, shape, deviation, most, cuts=(), held_as=jnp.bfloat16):
    factor_of = block_scale(key, shape, cuts, -0.22, 0.18) if cuts else 1.0
    values = jax.random.normal(key, shape, jnp.float32) * deviation * factor_of
    return jnp.minimum(jnp.maximum(values, -most), most).astype(held_as)


def setup_inputs(seed: int = 0) -> dict:
    key_list = jax.random.split(jax.random.key(seed), 9)
    features = normal_values(key_list[0], (NODES, FEAT), 1.0, 6.0, ((0, 32),))
    tiles = normal_values(key_list[1], (N_BLK, N_REP * SLOTS, TILE, TILE), (4 * TILE) ** -0.5, 0.25, ((0, 8), (1, 4)))
    tile_rows = place_ends(jax.random.randint(key_list[2], (N_BLK, N_REP * SLOTS), 0, N_REP * TPD), jax.random.fold_in(key_list[2], 1), 0, (N_REP * TPD) - 1).astype(jnp.int32)
    tile_cols = place_ends(jax.random.randint(key_list[3], (N_BLK, N_REP * SLOTS), 0, N_BLK * TPD), jax.random.fold_in(key_list[3], 1), 0, (N_BLK * TPD) - 1).astype(jnp.int32)
    counts = place_ends(jax.random.randint(key_list[4], (N_BLK, N_REP), SLOTS // 4, SLOTS + 1), jax.random.fold_in(key_list[4], 1), SLOTS // 4, SLOTS).astype(jnp.int32)
    weight = normal_values(key_list[5], (FEAT, FEAT), FEAT ** -0.5, 0.375)
    bias = normal_values(key_list[6], (FEAT,), 0.5, 3.0, (), jnp.float32)
    cotangent = normal_values(key_list[7], (NODES, FEAT), 1.0, 6.0, ((0, 32),))
    return {"features": features, "tiles": tiles, "tile_rows": tile_rows, "tile_cols": tile_cols, "counts": counts, "weight": weight, "bias": bias, "cotangent": cotangent}


def reference(features, tiles, tile_rows, tile_cols, counts, weight, bias, cotangent):
    highest = lax.Precision.HIGHEST
    tile_total = NODES // TILE
    feature_tiles = features.reshape(tile_total, TILE, FEAT).astype(jnp.float32)
    blocks = tiles.reshape(N_BLK, N_REP, SLOTS, TILE, TILE)
    slot_rows = tile_rows.reshape(N_BLK, N_REP, SLOTS)
    slot_cols = tile_cols.reshape(N_BLK, N_REP, SLOTS)
    slot_live = (jnp.arange(SLOTS, dtype=jnp.int32)[None, None, :] < counts[:, :, None]).astype(jnp.float32)
    rep_ids = jnp.arange(N_REP, dtype=jnp.int32)[None, :, None]
    blk_ids = jnp.arange(N_BLK, dtype=jnp.int32)[:, None, None]
    global_cols = (((slot_cols // TPD) * N_REP + rep_ids) * TPD + slot_cols % TPD).astype(jnp.int32)
    global_rows = (blk_ids * (N_REP * TPD) + slot_rows).astype(jnp.int32)

    def forward_group(running, group_index):
        chosen = feature_tiles[global_cols[group_index]]
        partial_value = jnp.einsum('rsij,rsjf->rsif', blocks[group_index].astype(jnp.float32), chosen, precision=highest)
        partial_value = partial_value * slot_live[group_index][:, :, None, None]
        running = running.at[global_rows[group_index].reshape(-1)].add(partial_value.reshape(N_REP * SLOTS, TILE, FEAT))
        return running, None

    start_zeros = jnp.zeros((tile_total, TILE, FEAT), jnp.float32)
    aggregate = lax.scan(forward_group, start_zeros, jnp.arange(N_BLK, dtype=jnp.int32))[0]
    aggregate = aggregate.reshape(NODES, FEAT).astype(jnp.bfloat16)
    pre_act = jnp.dot(aggregate, weight, preferred_element_type=jnp.float32) + bias.astype(jnp.float32)
    logistic = jax.nn.sigmoid(pre_act)
    activations = (pre_act * logistic).astype(jnp.bfloat16)
    act_grad = (cotangent.astype(jnp.float32) * logistic * (1.0 + pre_act * (1.0 - logistic))).astype(jnp.bfloat16)
    scale_factor = 1.0 / (N_BLK * N_REP)
    weight_grad = jnp.dot(aggregate.T, act_grad, preferred_element_type=jnp.float32) * scale_factor
    bias_grad = jnp.sum(act_grad.astype(jnp.float32), axis=0) * scale_factor
    agg_grad = jnp.dot(act_grad, weight.T, preferred_element_type=jnp.float32).astype(jnp.bfloat16)
    grad_tiles = agg_grad.reshape(tile_total, TILE, FEAT).astype(jnp.float32)

    def backward_group(running, group_index):
        chosen = grad_tiles[global_rows[group_index]]
        contribution = jnp.einsum('rsij,rsif->rsjf', blocks[group_index].astype(jnp.float32), chosen, precision=highest)
        contribution = contribution * slot_live[group_index][:, :, None, None]
        running = running.at[global_cols[group_index].reshape(-1)].add(contribution.reshape(N_REP * SLOTS, TILE, FEAT))
        return running, None

    feature_grad = lax.scan(backward_group, start_zeros, jnp.arange(N_BLK, dtype=jnp.int32))[0]
    feature_grad = feature_grad.reshape(NODES, FEAT).astype(jnp.bfloat16)
    return activations, feature_grad, weight_grad, bias_grad
```

```python
import functools

import jax
import jax.numpy as jnp
from jax import lax
from jax.experimental import pallas as pl
from jax.experimental.pallas import tpu as pltpu
from jax.sharding import PartitionSpec as P

MESH = pl.DeviceIdType.MESH
F32 = jnp.float32
BF16 = jnp.bfloat16


def flip(index, bits):
    out = index
    bit = 1
    while bit <= bits:
        if bits & bit:
            out = out + bit - 2 * bit * ((index // bit) % 2)
        bit *= 2
    return out


def kernel(n, R, T, S, features, tiles, rows, cols, counts, weight, bias, cotangent,
           act_out, fgrad_out, wgrad_out, bgrad_out,
           feat, tile_v, weight_v, cot_v, prod, send_b, recv_b, grads,
           send_d1, recv_d1, send_d2, recv_d2,
           send_w1, recv_w1, send_w2, recv_w2, slab_w3, slab_w4,
           load_sem, az_send, az_recv, ay_send, ay_recv, b_send, b_recv, c_send, c_recv,
           d1_send, d1_recv, d2_send, d2_recv, w1_send, w1_recv, w2_send, w2_recv,
           w3_send, w3_recv, w4_send, w4_recv):
    b = lax.axis_index("blk")
    r = lax.axis_index("rep")
    half = n // 2
    size = tiles.shape[1]
    width = weight.shape[1]
    fr = send_w1.shape[1] - 8
    fb = fr // n
    cb = send_w2.shape[1] - 8
    partner = flip(b, 1)

    def remote(src, dst, ssem, rsem, device):
        return pltpu.make_async_remote_copy(
            src_ref=src, dst_ref=dst, send_sem=ssem, recv_sem=rsem,
            device_id=device, device_id_type=MESH)

    loads = [
        pltpu.make_async_copy(features, feat.at[pl.ds(b * T, T)], load_sem.at[0]),
        pltpu.make_async_copy(tiles, tile_v, load_sem.at[1]),
        pltpu.make_async_copy(weight, weight_v, load_sem.at[2]),
        pltpu.make_async_copy(cotangent, cot_v, load_sem.at[3]),
    ]
    for c in loads:
        c.start()

    barrier = pltpu.get_barrier_semaphore()
    for s in range(1, n):
        pl.semaphore_signal(barrier, inc=1, device_id=(flip(b, s), r), device_id_type=MESH)
    for s in range(1, R):
        pl.semaphore_signal(barrier, inc=1, device_id=(b, flip(r, s)), device_id_type=MESH)
    pl.semaphore_wait(barrier, n - 1 + R - 1)

    mine = feat.at[pl.ds(b * T, T)]
    loads[0].wait()
    az = [None] * half
    order = sorted(range(1, half), key=lambda q: (q.bit_count(), q))
    ay = [None] * half
    ay[0] = remote(mine, mine, ay_send.at[0], ay_recv.at[0], (partner, r))
    ay[0].start()
    for q in order:
        az[q] = remote(mine, mine, az_send.at[q], az_recv.at[q], (flip(b, 2 * q), r))
        az[q].start()
    for q in order:
        az[q].wait_recv()
        block = feat.at[pl.ds(flip(b, 2 * q) * T, T)]
        ay[q] = remote(block, block, ay_send.at[q], ay_recv.at[q], (partner, r))
        ay[q].start()
    loads[1].wait()
    for q in [0] + order:
        ay[q].wait_recv()

    live = [lax.convert_element_type(k < counts[0, 0], F32) for k in range(S)]
    row_of = [rows[0, k] for k in range(S)]
    col_of = [cols[0, k] for k in range(S)]

    for k in range(S):
        prod[k] = jnp.dot(tile_v[k], feat[col_of[k]], preferred_element_type=F32)

    step = 32

    def combine(index_of, target, dest):
        w = [jnp.where(index_of[k] == target, live[k], 0.0) for k in range(S)]

        def chunk(i, carry):
            at = pl.multiple_of(i * step, step)
            total = prod[0, pl.ds(at, step), :] * w[0]
            for k in range(1, S):
                total = total + prod[k, pl.ds(at, step), :] * w[k]
            dest(at, total)
            return carry

        lax.fori_loop(0, size // step, chunk, 0)

    bs = {}
    peers = sorted(range(1, R), key=lambda s: (-(s // 2), s))
    for s in peers:
        peer = flip(r, s)
        for t in range(T):
            def put(at, value, t=t, s=s):
                send_b[s, t, pl.ds(at, step), :] = value.astype(BF16)
            combine(row_of, peer * T + t, put)
        bs[s] = remote(send_b.at[s], recv_b.at[s], b_send.at[s], b_recv.at[s], (b, peer))
        bs[s].start()
    own_value = []
    for t in range(T):
        w = [jnp.where(row_of[k] == r * T + t, live[k], 0.0) for k in range(S)]
        total = prod[0] * w[0]
        for k in range(1, S):
            total = total + prod[k] * w[k]
        own_value.append(total)
    total = jnp.concatenate(own_value, axis=0)
    loads[2].wait()
    loads[3].wait()
    for s in peers[::-1]:
        bs[s].wait_recv()
        total = total + recv_b[s].reshape(T * size, width).astype(F32)
    agg = total.astype(BF16)
    pre = jnp.dot(agg, weight_v[...], preferred_element_type=F32) + bias[...]
    sig = jax.nn.sigmoid(pre)
    act_grad = (cot_v[...].astype(F32) * sig * (1.0 + pre * (1.0 - sig))).astype(BF16)
    grad = lax.dot_general(act_grad, weight_v[...], (((1,), (1,)), ((), ())),
                           preferred_element_type=F32).astype(BF16)
    here = grads.at[pl.ds(r * T, T)]
    grads[pl.ds(r * T, T)] = grad.reshape(T, size, width)
    cs = {}
    for s in peers:
        cs[s] = remote(here, here, c_send.at[s], c_recv.at[s], (b, flip(r, s)))
        cs[s].start()

    act_out[...] = (pre * sig).astype(BF16)
    part = lax.dot_general(agg, act_grad, (((0,), (0,)), ((), ())), preferred_element_type=F32)
    bias_part = jnp.sum(act_grad.astype(F32).reshape(-1, 8, width), axis=0)
    for q in range(R):
        send_w1[q, :fr, :] = part[q * fr:(q + 1) * fr, :]
        send_w1[q, fr:, :] = bias_part
    w1 = {}
    for s in peers:
        peer = flip(r, s)
        w1[s] = remote(send_w1.at[peer], recv_w1.at[r], w1_send.at[s], w1_recv.at[s], (b, peer))
        w1[s].start()
    recv_w1[r] = send_w1[r]

    for s in peers:
        cs[s].wait_recv()
    for k in range(S):
        prod[k] = lax.dot_general(tile_v[k], grads[row_of[k]], (((0,), (0,)), ((), ())),
                                  preferred_element_type=F32)

    far = order[::-1]
    d1 = {}
    for q in far + [0]:
        goal = flip(partner, 2 * q)
        for t in range(T):
            def put(at, value, t=t, q=q):
                send_d1[q, t, pl.ds(at, step), :] = value.astype(BF16)
            combine(col_of, goal * T + t, put)
        d1[q] = remote(send_d1.at[q], recv_d1.at[q], d1_send.at[q], d1_recv.at[q], (partner, r))
        d1[q].start()

    for s in peers:
        w1[s].wait_recv()
    summed = recv_w1[0]
    for q in range(1, R):
        summed = summed + recv_w1[q]
    for j in range(n):
        send_w2[j, :fb, :] = summed[j * fb:(j + 1) * fb, :]
        send_w2[j, cb:, :] = summed[fr:, :]
    w2 = {}
    for s in range(1, n):
        peer = flip(b, s)
        w2[s] = remote(send_w2.at[peer], recv_w2.at[b], w2_send.at[s], w2_recv.at[s], (peer, r))
        w2[s].start()
    recv_w2[b] = send_w2[b]

    d2 = {}
    for q in far:
        goal = flip(b, 2 * q)
        d1[q].wait_recv()
        for t in range(T):
            def put(at, value, t=t, q=q):
                other = recv_d1[q, t, pl.ds(at, step), :].astype(F32)
                send_d2[q, t, pl.ds(at, step), :] = (value + other).astype(BF16)
            combine(col_of, goal * T + t, put)
        d2[q] = remote(send_d2.at[q], recv_d2.at[q], d2_send.at[q], d2_recv.at[q], (goal, r))
        d2[q].start()

    scale = 1.0 / (n * R)
    for s in range(1, n):
        w2[s].wait_recv()
    summed = recv_w2[0]
    for j in range(1, n):
        summed = summed + recv_w2[j]
    bgrad_out[...] = jnp.sum(summed[cb:, :], axis=0, keepdims=True) * scale
    slab_w3[b] = summed[:cb, :] * scale
    w3 = {}
    for s in range(1, n):
        w3[s] = remote(slab_w3.at[b], slab_w3.at[b], w3_send.at[s], w3_recv.at[s], (flip(b, s), r))
        w3[s].start()

    d1[0].wait_recv()
    for s in range(1, n):
        w3[s].wait_recv()
    for j in range(n):
        slab_w4[r, j * fb:(j + 1) * fb, :] = slab_w3[j, :fb, :]
    w4 = {}
    for s in peers:
        w4[s] = remote(slab_w4.at[r], slab_w4.at[r], w4_send.at[s], w4_recv.at[s], (b, flip(r, s)))
        w4[s].start()

    for q in far:
        d2[q].wait_recv()
    for t in range(T):
        def put(at, value, t=t):
            value = value + recv_d1[0, t, pl.ds(at, step), :].astype(F32)
            for q in far:
                value = value + recv_d2[q, t, pl.ds(at, step), :].astype(F32)
            fgrad_out[pl.ds(t * size + at, step), :] = value.astype(BF16)
        combine(col_of, b * T + t, put)

    for s in peers:
        w4[s].wait_recv()
    for q in range(R):
        wgrad_out[q * fr:(q + 1) * fr, :] = slab_w4[q]

    for group in (az[1:], ay, bs.values(), cs.values(), d1.values(), d2.values(),
                  w1.values(), w2.values(), w3.values(), w4.values()):
        for c in group:
            c.wait_send()


def per_device(n, R, features, tiles, tile_rows, tile_cols, counts, weight, bias, cotangent):
    own_rows, width = features.shape
    S, size = tiles.shape[1], tiles.shape[2]
    T = own_rows // size
    half = n // 2
    fr = weight.shape[0] // R
    fb = fr // n
    cb = max(8, fb)
    any_spec = pl.BlockSpec(memory_space=pl.ANY)
    smem = pl.BlockSpec(memory_space=pltpu.SMEM)
    vmem = pl.BlockSpec(memory_space=pltpu.VMEM)
    block = (T, size, width)
    dma = pltpu.SemaphoreType.DMA
    scratch = [
        pltpu.VMEM((n * T, size, width), BF16),
        pltpu.VMEM((S, size, size), BF16),
        pltpu.VMEM(weight.shape, BF16),
        pltpu.VMEM((own_rows, width), BF16),
        pltpu.VMEM((S, size, width), F32),
        pltpu.VMEM((R,) + block, BF16),
        pltpu.VMEM((R,) + block, BF16),
        pltpu.VMEM((R * T, size, width), BF16),
    ] + [pltpu.VMEM((half,) + block, BF16)] * 4 + [
        pltpu.VMEM((R, fr + 8, width), F32),
        pltpu.VMEM((R, fr + 8, width), F32),
        pltpu.VMEM((n, cb + 8, width), F32),
        pltpu.VMEM((n, cb + 8, width), F32),
        pltpu.VMEM((n, cb, width), F32),
        pltpu.VMEM((R, fr, width), F32),
        dma((4,)),
    ] + [dma((half,))] * 4 + [dma((R,))] * 4 + [dma((half,))] * 4 + [
        dma((R,)), dma((R,)), dma((n,)), dma((n,)), dma((n,)), dma((n,)), dma((R,)), dma((R,)),
    ]
    act, fgrad, wgrad, bgrad = pl.pallas_call(
        functools.partial(kernel, n, R, T, S),
        out_shape=(
            jax.ShapeDtypeStruct((own_rows, width), BF16),
            jax.ShapeDtypeStruct((own_rows, width), BF16),
            jax.ShapeDtypeStruct(weight.shape, F32),
            jax.ShapeDtypeStruct((1, width), F32),
        ),
        in_specs=[any_spec, any_spec, smem, smem, smem, any_spec, vmem, any_spec],
        out_specs=(vmem, vmem, vmem, vmem),
        scratch_shapes=scratch,
        compiler_params=pltpu.CompilerParams(
            collective_id=0, has_side_effects=True, vmem_limit_bytes=48 * 1024 * 1024),
        name="graph_layer",
    )(features.reshape(block), tiles[0], tile_rows, tile_cols, counts, weight,
      bias.reshape(1, -1), cotangent)
    return act, fgrad, wgrad, bgrad[0]


def solution(mesh):
    in_specs = (
        P(("blk", "rep"), None),
        P("blk", "rep", None, None),
        P("blk", "rep"),
        P("blk", "rep"),
        P("blk", "rep"),
        P(),
        P(),
        P(("blk", "rep"), None),
    )
    out_specs = (P(("blk", "rep"), None), P(("blk", "rep"), None), P(), P())
    body = functools.partial(per_device, mesh.shape["blk"], mesh.shape["rep"])
    return jax.shard_map(body, mesh=mesh, in_specs=in_specs, out_specs=out_specs, check_vma=False)
```

```python
import functools

import jax
import jax.numpy as jnp
from jax import lax
from jax.experimental import pallas as pl
from jax.experimental.pallas import tpu as pltpu
from jax.sharding import PartitionSpec as P

MESH = pl.DeviceIdType.MESH
F32 = jnp.float32
BF16 = jnp.bfloat16
VMEM_LIMIT = 63 * 1024 * 1024


def flip(index, bits):
    out = index
    bit = 1
    while bit <= bits:
        if bits & bit:
            out = out + bit - 2 * bit * ((index // bit) % 2)
        bit *= 2
    return out


def kernel(n, R, T, S, features, tiles, rows_in, cols_in, counts_in, weight, bias_in, cotangent,
           act_out, fgrad_out, wgrad_out, bgrad_out,
           rows, cols, counts, bias, feat, tile_v, weight_v, cot_v, prod, send_b, recv_b, grads,
           send_d1, recv_d1, send_d2, recv_d2,
           send_w1, recv_w1, send_w2, recv_w2, slab_w3, slab_w4,
           load_sem, az_send, az_recv, ay_send, ay_recv, b_send, b_recv, c_send, c_recv,
           d1_send, d1_recv, d2_send, d2_recv, w1_send, w1_recv, w2_send, w2_recv,
           w3_send, w3_recv, w4_send, w4_recv):
    b = lax.axis_index("blk")
    r = lax.axis_index("rep")
    half = n // 2
    size = tiles.shape[1]
    width = weight.shape[1]
    fb = weight.shape[0] // n
    fr = fb // R
    cb = send_w1.shape[1] - 16
    cr = send_w2.shape[1] - 8
    partner = flip(b, 1)

    def remote(src, dst, ssem, rsem, device):
        return pltpu.make_async_remote_copy(
            src_ref=src, dst_ref=dst, send_sem=ssem, recv_sem=rsem,
            device_id=device, device_id_type=MESH)

    loads = [
        pltpu.make_async_copy(features, feat.at[pl.ds(b * T, T)], load_sem.at[0]),
        pltpu.make_async_copy(tiles, tile_v, load_sem.at[1]),
        pltpu.make_async_copy(weight, weight_v, load_sem.at[2]),
        pltpu.make_async_copy(cotangent, cot_v, load_sem.at[3]),
        pltpu.make_async_copy(rows_in, rows, load_sem.at[4]),
        pltpu.make_async_copy(cols_in, cols, load_sem.at[5]),
        pltpu.make_async_copy(counts_in, counts, load_sem.at[6]),
        pltpu.make_async_copy(bias_in, bias, load_sem.at[7]),
    ]
    for c in loads:
        c.start()

    barrier = pltpu.get_barrier_semaphore()
    for s in range(1, n):
        pl.semaphore_signal(barrier, inc=1, device_id=(flip(b, s), r), device_id_type=MESH)
    for s in range(1, R):
        pl.semaphore_signal(barrier, inc=1, device_id=(b, flip(r, s)), device_id_type=MESH)
    pl.semaphore_wait(barrier, n - 1 + R - 1)

    loads[0].wait()
    order = sorted(range(1, half), key=lambda q: (q.bit_count(), q))
    own = [feat.at[b * T + t] for t in range(T)]
    az, ay = {}, {}
    for t in range(T):
        ay[0, t] = remote(own[t], own[t], ay_send.at[0, t], ay_recv.at[0, t], (partner, r))
        ay[0, t].start()
    for q in order:
        for t in range(T):
            az[q, t] = remote(own[t], own[t], az_send.at[q, t], az_recv.at[q, t],
                              (flip(b, 2 * q), r))
            az[q, t].start()
    for q in order:
        for t in range(T):
            az[q, t].wait_recv()
            tile = feat.at[flip(b, 2 * q) * T + t]
            ay[q, t] = remote(tile, tile, ay_send.at[q, t], ay_recv.at[q, t], (partner, r))
            ay[q, t].start()
    for c in loads[1:]:
        c.wait()
    for q in [0] + order:
        for t in range(T):
            ay[q, t].wait_recv()

    live = [lax.convert_element_type(k < counts[0, 0], F32) for k in range(S)]
    row_of = [rows[0, k] for k in range(S)]
    col_of = [cols[0, k] for k in range(S)]

    for k in range(S):
        prod[k] = jnp.dot(tile_v[k], feat[col_of[k]], preferred_element_type=F32)

    step = 32

    def combine(index_of, target, dest):
        w = [jnp.where(index_of[k] == target, live[k], 0.0) for k in range(S)]

        def chunk(i, carry):
            at = pl.multiple_of(i * step, step)
            total = prod[0, pl.ds(at, step), :] * w[0]
            for k in range(1, S):
                total = total + prod[k, pl.ds(at, step), :] * w[k]
            dest(at, total)
            return carry

        lax.fori_loop(0, size // step, chunk, 0)

    bs = {}
    peers = sorted(range(1, R), key=lambda s: (-(s // 2), s))
    for s in peers:
        peer = flip(r, s)
        for t in range(T):
            def put(at, value, t=t, s=s):
                send_b[s, t, pl.ds(at, step), :] = value.astype(BF16)
            combine(row_of, peer * T + t, put)
        bs[s] = remote(send_b.at[s], recv_b.at[s], b_send.at[s], b_recv.at[s], (b, peer))
        bs[s].start()
    own_value = []
    for t in range(T):
        w = [jnp.where(row_of[k] == r * T + t, live[k], 0.0) for k in range(S)]
        total = prod[0] * w[0]
        for k in range(1, S):
            total = total + prod[k] * w[k]
        own_value.append(total)
    total = jnp.concatenate(own_value, axis=0)
    for s in peers[::-1]:
        bs[s].wait_recv()
        total = total + recv_b[s].reshape(T * size, width).astype(F32)
    agg = total.astype(BF16)
    pre = jnp.dot(agg, weight_v[...], preferred_element_type=F32) + bias[...]
    sig = jax.nn.sigmoid(pre)
    act_grad = (cot_v[...].astype(F32) * sig * (1.0 + pre * (1.0 - sig))).astype(BF16)
    grad = lax.dot_general(act_grad, weight_v[...], (((1,), (1,)), ((), ())),
                           preferred_element_type=F32).astype(BF16)
    here = grads.at[pl.ds(r * T, T)]
    grads[pl.ds(r * T, T)] = grad.reshape(T, size, width)
    cs = {}
    for s in peers:
        cs[s] = remote(here, here, c_send.at[s], c_recv.at[s], (b, flip(r, s)))
        cs[s].start()

    part = lax.dot_general(agg, act_grad, (((0,), (0,)), ((), ())), preferred_element_type=F32)
    bias_part = jnp.sum(act_grad.astype(F32).reshape(-1, 16, width), axis=0).astype(BF16)
    part = part.astype(BF16)
    for q in range(n):
        send_w1[q, :fb, :] = part[q * fb:(q + 1) * fb, :]
        send_w1[q, cb:, :] = bias_part
    w1 = {}
    for s in range(1, n):
        peer = flip(b, s)
        w1[s] = remote(send_w1.at[peer], recv_w1.at[b], w1_send.at[s], w1_recv.at[s], (peer, r))
        w1[s].start()
    recv_w1[b] = send_w1[b]
    act_out[...] = (pre * sig).astype(BF16)

    for s in peers:
        cs[s].wait_recv()
    for k in range(S):
        prod[k] = lax.dot_general(tile_v[k], grads[row_of[k]], (((0,), (0,)), ((), ())),
                                  preferred_element_type=F32)

    far = order[::-1]
    d1, d2, w2, w3, w4 = {}, {}, {}, {}, {}

    def to_partner(q):
        goal = flip(partner, 2 * q)
        for t in range(T):
            def put(at, value, t=t, q=q):
                send_d1[q, t, pl.ds(at, step), :] = value.astype(BF16)
            combine(col_of, goal * T + t, put)
            d1[q, t] = remote(send_d1.at[q, t], recv_d1.at[q, t], d1_send.at[q, t],
                              d1_recv.at[q, t], (partner, r))
            d1[q, t].start()

    def to_owner(q):
        goal = flip(b, 2 * q)
        for t in range(T):
            def put(at, value, t=t, q=q):
                other = recv_d1[q, t, pl.ds(at, step), :].astype(F32)
                send_d2[q, t, pl.ds(at, step), :] = (value + other).astype(BF16)
            d1[q, t].wait_recv()
            combine(col_of, goal * T + t, put)
            d2[q, t] = remote(send_d2.at[q, t], recv_d2.at[q, t], d2_send.at[q, t],
                              d2_recv.at[q, t], (goal, r))
            d2[q, t].start()

    def weights_over_rep():
        for s in range(1, n):
            w1[s].wait_recv()
        total = recv_w1[0].astype(F32)
        for q in range(1, n):
            total = total + recv_w1[q].astype(F32)
        biases = total[cb:cb + 8, :] + total[cb + 8:, :]
        for j in range(R):
            send_w2[j, :fr, :] = total[j * fr:(j + 1) * fr, :]
            send_w2[j, cr:, :] = biases
        for s in peers:
            peer = flip(r, s)
            w2[s] = remote(send_w2.at[peer], recv_w2.at[r], w2_send.at[s], w2_recv.at[s],
                           (b, peer))
            w2[s].start()
        recv_w2[r] = send_w2[r]

    scale = 1.0 / (n * R)

    def weights_back():
        for s in peers:
            w2[s].wait_recv()
        total = recv_w2[0]
        for j in range(1, R):
            total = total + recv_w2[j]
        bgrad_out[...] = jnp.sum(total[cr:, :], axis=0, keepdims=True) * scale
        slab_w3[b] = total[:cr, :] * scale
        for s in range(1, n):
            w3[s] = remote(slab_w3.at[b], slab_w3.at[b], w3_send.at[s], w3_recv.at[s],
                           (flip(b, s), r))
            w3[s].start()

    to_partner(far[0])
    weights_over_rep()
    for q in far[1:]:
        to_partner(q)
    weights_back()
    to_partner(0)
    for q in far:
        to_owner(q)

    for s in range(1, n):
        w3[s].wait_recv()
    for s in peers:
        w4[s] = remote(slab_w3, slab_w4.at[r], w4_send.at[s], w4_recv.at[s], (b, flip(r, s)))
        w4[s].start()
    slab_w4[r] = slab_w3[...]

    for t in range(T):
        d1[0, t].wait_recv()
        for q in far:
            d2[q, t].wait_recv()

        def put(at, value, t=t):
            value = value + recv_d1[0, t, pl.ds(at, step), :].astype(F32)
            for q in far:
                value = value + recv_d2[q, t, pl.ds(at, step), :].astype(F32)
            fgrad_out[pl.ds(t * size + at, step), :] = value.astype(BF16)
        combine(col_of, b * T + t, put)

    for s in peers:
        w4[s].wait_recv()
    for j in range(n):
        for q in range(R):
            wgrad_out[j * fb + q * fr:j * fb + (q + 1) * fr, :] = slab_w4[q, j, :fr, :]

    for group in (az.values(), ay.values(), bs.values(), cs.values(), d1.values(), d2.values(),
                  w1.values(), w2.values(), w3.values(), w4.values()):
        for c in group:
            c.wait_send()


def per_device(n, R, features, tiles, tile_rows, tile_cols, counts, weight, bias, cotangent):
    own_rows, width = features.shape
    S, size = tiles.shape[1], tiles.shape[2]
    T = own_rows // size
    half = n // 2
    fb = weight.shape[0] // n
    fr = fb // R
    cb, cr = max(16, fb), max(8, fr)
    hbm = pl.BlockSpec(memory_space=pltpu.HBM)
    vmem = pl.BlockSpec(memory_space=pltpu.VMEM)
    block = (T, size, width)
    dma = pltpu.SemaphoreType.DMA
    scratch = [
        pltpu.SMEM(tile_rows.shape, jnp.int32),
        pltpu.SMEM(tile_cols.shape, jnp.int32),
        pltpu.SMEM(counts.shape, jnp.int32),
        pltpu.VMEM((1, width), F32),
        pltpu.VMEM((n * T, size, width), BF16),
        pltpu.VMEM((S, size, size), BF16),
        pltpu.VMEM(weight.shape, BF16),
        pltpu.VMEM((own_rows, width), BF16),
        pltpu.VMEM((S, size, width), F32),
        pltpu.VMEM((R,) + block, BF16),
        pltpu.VMEM((R,) + block, BF16),
        pltpu.VMEM((R * T, size, width), BF16),
    ] + [pltpu.VMEM((half,) + block, BF16)] * 4 + [
        pltpu.VMEM((n, cb + 16, width), BF16),
        pltpu.VMEM((n, cb + 16, width), BF16),
        pltpu.VMEM((R, cr + 8, width), F32),
        pltpu.VMEM((R, cr + 8, width), F32),
        pltpu.VMEM((n, cr, width), F32),
        pltpu.VMEM((R, n, cr, width), F32),
        dma((8,)),
    ] + [dma((half, T))] * 4 + [dma((R,))] * 4 + [dma((half, T))] * 4 + [
        dma((n,)), dma((n,)), dma((R,)), dma((R,)), dma((n,)), dma((n,)), dma((R,)), dma((R,)),
    ]
    act, fgrad, wgrad, bgrad = pl.pallas_call(
        functools.partial(kernel, n, R, T, S),
        out_shape=(
            jax.ShapeDtypeStruct((own_rows, width), BF16),
            jax.ShapeDtypeStruct((own_rows, width), BF16),
            jax.ShapeDtypeStruct(weight.shape, F32),
            jax.ShapeDtypeStruct((1, width), F32),
        ),
        in_specs=[hbm] * 8,
        out_specs=(vmem, vmem, vmem, vmem),
        scratch_shapes=scratch,
        compiler_params=pltpu.CompilerParams(
            collective_id=0, has_side_effects=True, vmem_limit_bytes=VMEM_LIMIT),
        name="graph_layer",
    )(features.reshape(block), tiles[0], tile_rows, tile_cols, counts, weight,
      bias.reshape(1, -1), cotangent)
    return act, fgrad, wgrad, bgrad[0]


def solution(mesh):
    in_specs = (
        P(("blk", "rep"), None),
        P("blk", "rep", None, None),
        P("blk", "rep"),
        P("blk", "rep"),
        P("blk", "rep"),
        P(),
        P(),
        P(("blk", "rep"), None),
    )
    out_specs = (P(("blk", "rep"), None), P(("blk", "rep"), None), P(), P())
    body = functools.partial(per_device, mesh.shape["blk"], mesh.shape["rep"])
    return jax.shard_map(body, mesh=mesh, in_specs=in_specs, out_specs=out_specs, check_vma=False)
```

```python
import functools

import jax
import jax.numpy as jnp
from jax import lax
from jax.experimental import pallas as pl
from jax.experimental.pallas import tpu as pltpu
from jax.sharding import PartitionSpec as P

MESH = pl.DeviceIdType.MESH
F32 = jnp.float32
BF16 = jnp.bfloat16
VMEM_LIMIT = 63 * 1024 * 1024


def flip(index, bits):
    out = index
    bit = 1
    while bit <= bits:
        if bits & bit:
            out = out + bit - 2 * bit * ((index // bit) % 2)
        bit *= 2
    return out


def kernel(n, R, T, S, features, tiles, rows_in, cols_in, counts_in, weight, bias_in, cotangent,
           act_out, fgrad_out, wgrad_out, bgrad_out,
           rows, cols, counts, bias, feat, tile_v, weight_v, cot_v, prod, total_v, send_b, recv_b, grads,
           send_d1, recv_d1, send_d2, recv_d2,
           send_w1, recv_w1, send_w2, recv_w2, slab_w3, slab_w4,
           load_sem, az_send, az_recv, ay_send, ay_recv, b_send, b_recv, c_send, c_recv,
           d1_send, d1_recv, d2_send, d2_recv, w1_send, w1_recv, w2_send, w2_recv,
           w3_send, w3_recv, w4_send, w4_recv):
    b = lax.axis_index("blk")
    r = lax.axis_index("rep")
    half = n // 2
    size = tiles.shape[1]
    width = weight.shape[1]
    fb = weight.shape[0] // n
    fr = fb // R
    cb = send_w1.shape[1] - 16
    cr = send_w2.shape[1] - 8
    partner = flip(b, 1)

    def remote(src, dst, ssem, rsem, device):
        return pltpu.make_async_remote_copy(
            src_ref=src, dst_ref=dst, send_sem=ssem, recv_sem=rsem,
            device_id=device, device_id_type=MESH)

    loads = [
        pltpu.make_async_copy(features, feat.at[pl.ds(b * T, T)], load_sem.at[0]),
        pltpu.make_async_copy(tiles, tile_v, load_sem.at[1]),
        pltpu.make_async_copy(weight, weight_v, load_sem.at[2]),
        pltpu.make_async_copy(cotangent, cot_v, load_sem.at[3]),
        pltpu.make_async_copy(rows_in, rows, load_sem.at[4]),
        pltpu.make_async_copy(cols_in, cols, load_sem.at[5]),
        pltpu.make_async_copy(counts_in, counts, load_sem.at[6]),
        pltpu.make_async_copy(bias_in, bias, load_sem.at[7]),
    ]
    for c in loads:
        c.start()

    barrier = pltpu.get_barrier_semaphore()
    for s in range(1, n):
        pl.semaphore_signal(barrier, inc=1, device_id=(flip(b, s), r), device_id_type=MESH)
    for s in range(1, R):
        pl.semaphore_signal(barrier, inc=1, device_id=(b, flip(r, s)), device_id_type=MESH)
    pl.semaphore_wait(barrier, n - 1 + R - 1)

    loads[0].wait()
    order = sorted(range(1, half), key=lambda q: (q.bit_count(), q))
    own = [feat.at[b * T + t] for t in range(T)]
    az, ay = {}, {}
    for t in range(T):
        ay[0, t] = remote(own[t], own[t], ay_send.at[0, t], ay_recv.at[0, t], (partner, r))
        ay[0, t].start()
    for q in order:
        for t in range(T):
            az[q, t] = remote(own[t], own[t], az_send.at[q, t], az_recv.at[q, t],
                              (flip(b, 2 * q), r))
            az[q, t].start()
    for q in order:
        for t in range(T):
            az[q, t].wait_recv()
            tile = feat.at[flip(b, 2 * q) * T + t]
            ay[q, t] = remote(tile, tile, ay_send.at[q, t], ay_recv.at[q, t], (partner, r))
            ay[q, t].start()
    for c in loads[1:]:
        c.wait()
    for q in [0] + order:
        for t in range(T):
            ay[q, t].wait_recv()

    live = [lax.convert_element_type(k < counts[0, 0], F32) for k in range(S)]
    row_of = [rows[0, k] for k in range(S)]
    col_of = [cols[0, k] for k in range(S)]

    for k in range(S):
        prod[k] = jnp.dot(tile_v[k], feat[col_of[k]], preferred_element_type=F32)

    step = 32

    def combine(index_of, target, dest):
        w = [jnp.where(index_of[k] == target, live[k], 0.0) for k in range(S)]

        def chunk(i, carry):
            at = pl.multiple_of(i * step, step)
            total = prod[0, pl.ds(at, step), :] * w[0]
            for k in range(1, S):
                total = total + prod[k, pl.ds(at, step), :] * w[k]
            dest(at, total)
            return carry

        lax.fori_loop(0, size // step, chunk, 0)

    bs, cs = {}, {}
    peers = sorted(range(1, R), key=lambda s: (-(s // 2), s))
    for t in range(T):
        for s in peers:
            peer = flip(r, s)

            def put(at, value, t=t, s=s):
                send_b[s, t, pl.ds(at, step), :] = value.astype(BF16)

            combine(row_of, peer * T + t, put)
            bs[s, t] = remote(send_b.at[s, t], recv_b.at[s, t], b_send.at[s, t],
                              b_recv.at[s, t], (b, peer))
            bs[s, t].start()
    for t in range(T):

        def put(at, value, t=t):
            total_v[t, pl.ds(at, step), :] = value

        combine(row_of, r * T + t, put)
    agg_parts, act_parts = [], []
    for t in range(T):
        total = total_v[t]
        for s in peers[::-1]:
            bs[s, t].wait_recv()
            total = total + recv_b[s, t].astype(F32)
        agg_t = total.astype(BF16)
        pre = jnp.dot(agg_t, weight_v[...], preferred_element_type=F32) + bias[...]
        sig = jax.nn.sigmoid(pre)
        cot_t = cot_v[t * size:(t + 1) * size, :].astype(F32)
        act_t = (cot_t * sig * (1.0 + pre * (1.0 - sig))).astype(BF16)
        grads[r * T + t] = lax.dot_general(
            act_t, weight_v[...], (((1,), (1,)), ((), ())),
            preferred_element_type=F32).astype(BF16)
        here = grads.at[r * T + t]
        for s in peers:
            cs[s, t] = remote(here, here, c_send.at[s, t], c_recv.at[s, t], (b, flip(r, s)))
            cs[s, t].start()
        act_out[t * size:(t + 1) * size, :] = (pre * sig).astype(BF16)
        agg_parts.append(agg_t)
        act_parts.append(act_t)
    agg = jnp.concatenate(agg_parts, axis=0)
    act_grad = jnp.concatenate(act_parts, axis=0)

    part = lax.dot_general(agg, act_grad, (((0,), (0,)), ((), ())), preferred_element_type=F32)
    bias_part = jnp.sum(act_grad.astype(F32).reshape(-1, 16, width), axis=0).astype(BF16)
    part = part.astype(BF16)
    for q in range(n):
        send_w1[q, :fb, :] = part[q * fb:(q + 1) * fb, :]
        send_w1[q, cb:, :] = bias_part
    w1 = {}
    for s in range(1, n):
        peer = flip(b, s)
        w1[s] = remote(send_w1.at[peer], recv_w1.at[b], w1_send.at[s], w1_recv.at[s], (peer, r))
        w1[s].start()
    recv_w1[b] = send_w1[b]

    for t in range(T):
        for s in peers:
            cs[s, t].wait_recv()
    for k in range(S):
        prod[k] = lax.dot_general(tile_v[k], grads[row_of[k]], (((0,), (0,)), ((), ())),
                                  preferred_element_type=F32)

    far = order[::-1]
    d1, d2, w2, w3, w4 = {}, {}, {}, {}, {}

    def to_partner(q):
        goal = flip(partner, 2 * q)
        for t in range(T):
            def put(at, value, t=t, q=q):
                send_d1[q, t, pl.ds(at, step), :] = value.astype(BF16)
            combine(col_of, goal * T + t, put)
            d1[q, t] = remote(send_d1.at[q, t], recv_d1.at[q, t], d1_send.at[q, t],
                              d1_recv.at[q, t], (partner, r))
            d1[q, t].start()

    def to_owner(q):
        goal = flip(b, 2 * q)
        for t in range(T):
            def put(at, value, t=t, q=q):
                other = recv_d1[q, t, pl.ds(at, step), :].astype(F32)
                send_d2[q, t, pl.ds(at, step), :] = (value + other).astype(BF16)
            d1[q, t].wait_recv()
            combine(col_of, goal * T + t, put)
            d2[q, t] = remote(send_d2.at[q, t], recv_d2.at[q, t], d2_send.at[q, t],
                              d2_recv.at[q, t], (goal, r))
            d2[q, t].start()

    def weights_over_rep():
        for s in range(1, n):
            w1[s].wait_recv()
        total = recv_w1[0].astype(F32)
        for q in range(1, n):
            total = total + recv_w1[q].astype(F32)
        biases = total[cb:cb + 8, :] + total[cb + 8:, :]
        for j in range(R):
            send_w2[j, :fr, :] = total[j * fr:(j + 1) * fr, :]
            send_w2[j, cr:, :] = biases
        for s in peers:
            peer = flip(r, s)
            w2[s] = remote(send_w2.at[peer], recv_w2.at[r], w2_send.at[s], w2_recv.at[s],
                           (b, peer))
            w2[s].start()
        recv_w2[r] = send_w2[r]

    scale = 1.0 / (n * R)

    def weights_back():
        for s in peers:
            w2[s].wait_recv()
        total = recv_w2[0]
        for j in range(1, R):
            total = total + recv_w2[j]
        bgrad_out[...] = jnp.sum(total[cr:, :], axis=0, keepdims=True) * scale
        slab_w3[b] = total[:cr, :] * scale
        for s in range(1, n):
            w3[s] = remote(slab_w3.at[b], slab_w3.at[b], w3_send.at[s], w3_recv.at[s],
                           (flip(b, s), r))
            w3[s].start()

    to_partner(far[0])
    weights_over_rep()
    for q in far[1:]:
        to_partner(q)
    weights_back()
    to_partner(0)
    for q in far:
        to_owner(q)

    for s in range(1, n):
        w3[s].wait_recv()
    for s in peers:
        w4[s] = remote(slab_w3, slab_w4.at[r], w4_send.at[s], w4_recv.at[s], (b, flip(r, s)))
        w4[s].start()
    slab_w4[r] = slab_w3[...]

    for t in range(T):
        d1[0, t].wait_recv()
        for q in far:
            d2[q, t].wait_recv()

        def put(at, value, t=t):
            value = value + recv_d1[0, t, pl.ds(at, step), :].astype(F32)
            for q in far:
                value = value + recv_d2[q, t, pl.ds(at, step), :].astype(F32)
            fgrad_out[pl.ds(t * size + at, step), :] = value.astype(BF16)
        combine(col_of, b * T + t, put)

    for s in peers:
        w4[s].wait_recv()
    for j in range(n):
        for q in range(R):
            wgrad_out[j * fb + q * fr:j * fb + (q + 1) * fr, :] = slab_w4[q, j, :fr, :]

    for group in (az.values(), ay.values(), bs.values(), cs.values(), d1.values(), d2.values(),
                  w1.values(), w2.values(), w3.values(), w4.values()):
        for c in group:
            c.wait_send()


def emit(a, f, w, g, a_out, f_out, w_out, g_out):
    a_out[...] = a[...]
    f_out[...] = f[...]
    w_out[...] = w[...]
    g_out[...] = g[...]


def per_device(n, R, features, tiles, tile_rows, tile_cols, counts, weight, bias, cotangent):
    own_rows, width = features.shape
    S, size = tiles.shape[1], tiles.shape[2]
    T = own_rows // size
    half = n // 2
    fb = weight.shape[0] // n
    fr = fb // R
    cb, cr = max(16, fb), max(8, fr)
    hbm = pl.BlockSpec(memory_space=pltpu.HBM)
    vmem = pl.BlockSpec(memory_space=pltpu.VMEM)
    block = (T, size, width)
    dma = pltpu.SemaphoreType.DMA
    scratch = [
        pltpu.SMEM(tile_rows.shape, jnp.int32),
        pltpu.SMEM(tile_cols.shape, jnp.int32),
        pltpu.SMEM(counts.shape, jnp.int32),
        pltpu.VMEM((1, width), F32),
        pltpu.VMEM((n * T, size, width), BF16),
        pltpu.VMEM((S, size, size), BF16),
        pltpu.VMEM(weight.shape, BF16),
        pltpu.VMEM((own_rows, width), BF16),
        pltpu.VMEM((S, size, width), F32),
        pltpu.VMEM(block, F32),
        pltpu.VMEM((R,) + block, BF16),
        pltpu.VMEM((R,) + block, BF16),
        pltpu.VMEM((R * T, size, width), BF16),
    ] + [pltpu.VMEM((half,) + block, BF16)] * 4 + [
        pltpu.VMEM((n, cb + 16, width), BF16),
        pltpu.VMEM((n, cb + 16, width), BF16),
        pltpu.VMEM((R, cr + 8, width), F32),
        pltpu.VMEM((R, cr + 8, width), F32),
        pltpu.VMEM((n, cr, width), F32),
        pltpu.VMEM((R, n, cr, width), F32),
        dma((8,)),
    ] + [dma((half, T))] * 4 + [dma((R, T))] * 4 + [dma((half, T))] * 4 + [
        dma((n,)), dma((n,)), dma((R,)), dma((R,)), dma((n,)), dma((n,)), dma((R,)), dma((R,)),
    ]
    act, fgrad, wgrad, bgrad = pl.pallas_call(
        functools.partial(kernel, n, R, T, S),
        out_shape=(
            jax.ShapeDtypeStruct((own_rows, width), BF16),
            jax.ShapeDtypeStruct((own_rows, width), BF16),
            jax.ShapeDtypeStruct(weight.shape, F32),
            jax.ShapeDtypeStruct((1, width), F32),
        ),
        in_specs=[hbm] * 8,
        out_specs=(vmem, vmem, vmem, vmem),
        scratch_shapes=scratch,
        compiler_params=pltpu.CompilerParams(
            collective_id=0, has_side_effects=True, vmem_limit_bytes=VMEM_LIMIT),
        name="graph_layer",
    )(features.reshape(block), tiles[0], tile_rows, tile_cols, counts, weight,
      bias.reshape(1, -1), cotangent)
    results = pl.pallas_call(
        emit,
        out_shape=tuple(jax.ShapeDtypeStruct(x.shape, x.dtype)
                        for x in (act, fgrad, wgrad, bgrad)),
        in_specs=[vmem] * 4,
        out_specs=(vmem,) * 4,
        name="emit_results",
    )(act, fgrad, wgrad, bgrad)
    return results[0], results[1], results[2], results[3][0]


def solution(mesh):
    in_specs = (
        P(("blk", "rep"), None),
        P("blk", "rep", None, None),
        P("blk", "rep"),
        P("blk", "rep"),
        P("blk", "rep"),
        P(),
        P(),
        P(("blk", "rep"), None),
    )
    out_specs = (P(("blk", "rep"), None), P(("blk", "rep"), None), P(), P())
    body = functools.partial(per_device, mesh.shape["blk"], mesh.shape["rep"])
    return jax.shard_map(body, mesh=mesh, in_specs=in_specs, out_specs=out_specs, check_vma=False)
```

```python
import functools

import jax
import jax.numpy as jnp
from jax import lax
from jax.experimental import pallas as pl
from jax.experimental.pallas import tpu as pltpu
from jax.sharding import PartitionSpec as P

MESH = pl.DeviceIdType.MESH
F32 = jnp.float32
BF16 = jnp.bfloat16
VMEM_LIMIT = 63 * 1024 * 1024


def flip(index, bits):
    out = index
    bit = 1
    while bit <= bits:
        if bits & bit:
            out = out + bit - 2 * bit * ((index // bit) % 2)
        bit *= 2
    return out


def kernel(n, R, T, S, features, tiles, rows_in, cols_in, counts_in, weight, bias_in, cotangent,
           act_out, fgrad_out, wgrad_out, bgrad_out,
           rows, cols, counts, bias, feat, tile_v, weight_v, cot_v, prod, total_v, send_b, recv_b, grads,
           send_d1, recv_d1, send_d2, recv_d2,
           send_w1, recv_w1, send_w2, recv_w2, slab_w3, slab_w4,
           load_sem, az_send, az_recv, ay_send, ay_recv, b_send, b_recv, c_send, c_recv,
           d1_send, d1_recv, d2_send, d2_recv, w1_send, w1_recv, w2_send, w2_recv,
           w3_send, w3_recv, w4_send, w4_recv):
    b = lax.axis_index("blk")
    r = lax.axis_index("rep")
    half = n // 2
    size = tiles.shape[1]
    width = weight.shape[1]
    fb = weight.shape[0] // n
    fr = fb // R
    cb = send_w1.shape[1] - 16
    cr = send_w2.shape[1] - 8
    partner = flip(b, 1)

    def remote(src, dst, ssem, rsem, device):
        return pltpu.make_async_remote_copy(
            src_ref=src, dst_ref=dst, send_sem=ssem, recv_sem=rsem,
            device_id=device, device_id_type=MESH)

    loads = [
        pltpu.make_async_copy(features, feat.at[pl.ds(b * T, T)], load_sem.at[0]),
        pltpu.make_async_copy(tiles, tile_v, load_sem.at[1]),
        pltpu.make_async_copy(weight, weight_v, load_sem.at[2]),
        pltpu.make_async_copy(cotangent, cot_v, load_sem.at[3]),
        pltpu.make_async_copy(rows_in, rows, load_sem.at[4]),
        pltpu.make_async_copy(cols_in, cols, load_sem.at[5]),
        pltpu.make_async_copy(counts_in, counts, load_sem.at[6]),
        pltpu.make_async_copy(bias_in, bias, load_sem.at[7]),
    ]
    for c in loads:
        c.start()

    barrier = pltpu.get_barrier_semaphore()
    for s in range(1, n):
        pl.semaphore_signal(barrier, inc=1, device_id=(flip(b, s), r), device_id_type=MESH)
    for s in range(1, R):
        pl.semaphore_signal(barrier, inc=1, device_id=(b, flip(r, s)), device_id_type=MESH)
    pl.semaphore_wait(barrier, n - 1 + R - 1)

    loads[0].wait()
    order = sorted(range(1, half), key=lambda q: (q.bit_count(), q))
    own = [feat.at[b * T + t] for t in range(T)]
    az, ay = {}, {}
    for t in range(T):
        ay[0, t] = remote(own[t], own[t], ay_send.at[0, t], ay_recv.at[0, t], (partner, r))
        ay[0, t].start()
    for q in order:
        for t in range(T):
            az[q, t] = remote(own[t], own[t], az_send.at[q, t], az_recv.at[q, t],
                              (flip(b, 2 * q), r))
            az[q, t].start()
    for q in order:
        for t in range(T):
            az[q, t].wait_recv()
            tile = feat.at[flip(b, 2 * q) * T + t]
            ay[q, t] = remote(tile, tile, ay_send.at[q, t], ay_recv.at[q, t], (partner, r))
            ay[q, t].start()
    for c in loads[1:]:
        c.wait()
    for q in [0] + order:
        for t in range(T):
            ay[q, t].wait_recv()

    live = [lax.convert_element_type(k < counts[0, 0], F32) for k in range(S)]
    row_of = [rows[0, k] for k in range(S)]
    col_of = [cols[0, k] for k in range(S)]

    for k in range(S):
        prod[k] = jnp.dot(tile_v[k], feat[col_of[k]], preferred_element_type=F32)

    step = 32

    def combine(index_of, target, dest):
        w = [jnp.where(index_of[k] == target, live[k], 0.0) for k in range(S)]

        def chunk(i, carry):
            at = pl.multiple_of(i * step, step)
            total = prod[0, pl.ds(at, step), :] * w[0]
            for k in range(1, S):
                total = total + prod[k, pl.ds(at, step), :] * w[k]
            dest(at, total)
            return carry

        lax.fori_loop(0, size // step, chunk, 0)

    bs, cs = {}, {}
    peers = sorted(range(1, R), key=lambda s: (-(s // 2), s))
    for t in range(T):
        for s in peers:
            peer = flip(r, s)

            def put(at, value, t=t, s=s):
                send_b[s, t, pl.ds(at, step), :] = value.astype(BF16)

            combine(row_of, peer * T + t, put)
            bs[s, t] = remote(send_b.at[s, t], recv_b.at[s, t], b_send.at[s, t],
                              b_recv.at[s, t], (b, peer))
            bs[s, t].start()
    for t in range(T):

        def put(at, value, t=t):
            total_v[t, pl.ds(at, step), :] = value

        combine(row_of, r * T + t, put)
    agg_parts, act_parts = [], []
    for t in range(T):
        total = total_v[t]
        for s in peers[::-1]:
            bs[s, t].wait_recv()
            total = total + recv_b[s, t].astype(F32)
        agg_t = total.astype(BF16)
        pre = jnp.dot(agg_t, weight_v[...], preferred_element_type=F32) + bias[...]
        sig = jax.nn.sigmoid(pre)
        cot_t = cot_v[t * size:(t + 1) * size, :].astype(F32)
        act_t = (cot_t * sig * (1.0 + pre * (1.0 - sig))).astype(BF16)
        grads[r * T + t] = lax.dot_general(
            act_t, weight_v[...], (((1,), (1,)), ((), ())),
            preferred_element_type=F32).astype(BF16)
        here = grads.at[r * T + t]
        for s in [s for s in peers if s % 2 == 0] + [1]:
            cs[s, t] = remote(here, here, c_send.at[s, t], c_recv.at[s, t], (b, flip(r, s)))
            cs[s, t].start()
        act_out[t * size:(t + 1) * size, :] = (pre * sig).astype(BF16)
        agg_parts.append(agg_t)
        act_parts.append(act_t)
    agg = jnp.concatenate(agg_parts, axis=0)
    act_grad = jnp.concatenate(act_parts, axis=0)

    part = lax.dot_general(agg, act_grad, (((0,), (0,)), ((), ())), preferred_element_type=F32)
    bias_part = jnp.sum(act_grad.astype(F32).reshape(-1, 16, width), axis=0).astype(BF16)
    part = part.astype(BF16)
    for q in range(n):
        send_w1[q, :fb, :] = part[q * fb:(q + 1) * fb, :]
        send_w1[q, cb:, :] = bias_part
    w1 = {}
    for s in range(1, n):
        peer = flip(b, s)
        w1[s] = remote(send_w1.at[peer], recv_w1.at[b], w1_send.at[s], w1_recv.at[s], (peer, r))
        w1[s].start()
    recv_w1[b] = send_w1[b]

    for t in range(T):
        for s in peers:
            if s % 2 == 0:
                cs[s, t].wait_recv()
                block = grads.at[flip(r, s) * T + t]
                cs[s + 1, t] = remote(block, block, c_send.at[s + 1, t], c_recv.at[s + 1, t],
                                      (b, flip(r, 1)))
                cs[s + 1, t].start()
    for t in range(T):
        for s in peers:
            if s % 2 == 1:
                cs[s, t].wait_recv()
    for k in range(S):
        prod[k] = lax.dot_general(tile_v[k], grads[row_of[k]], (((0,), (0,)), ((), ())),
                                  preferred_element_type=F32)

    far = order[::-1]
    d1, d2, w2, w3, w4 = {}, {}, {}, {}, {}

    def to_partner(q):
        goal = flip(partner, 2 * q)
        for t in range(T):
            def put(at, value, t=t, q=q):
                send_d1[q, t, pl.ds(at, step), :] = value.astype(BF16)
            combine(col_of, goal * T + t, put)
            d1[q, t] = remote(send_d1.at[q, t], recv_d1.at[q, t], d1_send.at[q, t],
                              d1_recv.at[q, t], (partner, r))
            d1[q, t].start()

    def to_owner(q):
        goal = flip(b, 2 * q)
        for t in range(T):
            def put(at, value, t=t, q=q):
                other = recv_d1[q, t, pl.ds(at, step), :].astype(F32)
                send_d2[q, t, pl.ds(at, step), :] = (value + other).astype(BF16)
            d1[q, t].wait_recv()
            combine(col_of, goal * T + t, put)
            d2[q, t] = remote(send_d2.at[q, t], recv_d2.at[q, t], d2_send.at[q, t],
                              d2_recv.at[q, t], (goal, r))
            d2[q, t].start()

    def weights_over_rep():
        for s in range(1, n):
            w1[s].wait_recv()
        total = recv_w1[0].astype(F32)
        for q in range(1, n):
            total = total + recv_w1[q].astype(F32)
        biases = total[cb:cb + 8, :] + total[cb + 8:, :]
        for j in range(R):
            send_w2[j, :fr, :] = total[j * fr:(j + 1) * fr, :]
            send_w2[j, cr:, :] = biases
        for s in peers:
            peer = flip(r, s)
            w2[s] = remote(send_w2.at[peer], recv_w2.at[r], w2_send.at[s], w2_recv.at[s],
                           (b, peer))
            w2[s].start()
        recv_w2[r] = send_w2[r]

    scale = 1.0 / (n * R)

    def weights_back():
        for s in peers:
            w2[s].wait_recv()
        total = recv_w2[0]
        for j in range(1, R):
            total = total + recv_w2[j]
        bgrad_out[...] = jnp.sum(total[cr:, :], axis=0, keepdims=True) * scale
        slab_w3[b] = total[:cr, :] * scale
        for s in range(1, n):
            w3[s] = remote(slab_w3.at[b], slab_w3.at[b], w3_send.at[s], w3_recv.at[s],
                           (flip(b, s), r))
            w3[s].start()

    to_partner(far[0])
    weights_over_rep()
    for q in far[1:]:
        to_partner(q)
    weights_back()
    to_partner(0)
    for q in far:
        to_owner(q)

    for s in range(1, n):
        w3[s].wait_recv()
    for s in peers:
        w4[s] = remote(slab_w3, slab_w4.at[r], w4_send.at[s], w4_recv.at[s], (b, flip(r, s)))
        w4[s].start()
    slab_w4[r] = slab_w3[...]

    for t in range(T):
        d1[0, t].wait_recv()
        for q in far:
            d2[q, t].wait_recv()

        def put(at, value, t=t):
            value = value + recv_d1[0, t, pl.ds(at, step), :].astype(F32)
            for q in far:
                value = value + recv_d2[q, t, pl.ds(at, step), :].astype(F32)
            fgrad_out[pl.ds(t * size + at, step), :] = value.astype(BF16)
        combine(col_of, b * T + t, put)

    for s in peers:
        w4[s].wait_recv()
    for j in range(n):
        for q in range(R):
            wgrad_out[j * fb + q * fr:j * fb + (q + 1) * fr, :] = slab_w4[q, j, :fr, :]

    for group in (az.values(), ay.values(), bs.values(), cs.values(), d1.values(), d2.values(),
                  w1.values(), w2.values(), w3.values(), w4.values()):
        for c in group:
            c.wait_send()


def emit(a, f, w, g, a_out, f_out, w_out, g_out):
    a_out[...] = a[...]
    f_out[...] = f[...]
    w_out[...] = w[...]
    g_out[...] = g[...]


def per_device(n, R, features, tiles, tile_rows, tile_cols, counts, weight, bias, cotangent):
    own_rows, width = features.shape
    S, size = tiles.shape[1], tiles.shape[2]
    T = own_rows // size
    half = n // 2
    fb = weight.shape[0] // n
    fr = fb // R
    cb, cr = max(16, fb), max(8, fr)
    hbm = pl.BlockSpec(memory_space=pltpu.HBM)
    vmem = pl.BlockSpec(memory_space=pltpu.VMEM)
    block = (T, size, width)
    dma = pltpu.SemaphoreType.DMA
    scratch = [
        pltpu.SMEM(tile_rows.shape, jnp.int32),
        pltpu.SMEM(tile_cols.shape, jnp.int32),
        pltpu.SMEM(counts.shape, jnp.int32),
        pltpu.VMEM((1, width), F32),
        pltpu.VMEM((n * T, size, width), BF16),
        pltpu.VMEM((S, size, size), BF16),
        pltpu.VMEM(weight.shape, BF16),
        pltpu.VMEM((own_rows, width), BF16),
        pltpu.VMEM((S, size, width), F32),
        pltpu.VMEM(block, F32),
        pltpu.VMEM((R,) + block, BF16),
        pltpu.VMEM((R,) + block, BF16),
        pltpu.VMEM((R * T, size, width), BF16),
    ] + [pltpu.VMEM((half,) + block, BF16)] * 4 + [
        pltpu.VMEM((n, cb + 16, width), BF16),
        pltpu.VMEM((n, cb + 16, width), BF16),
        pltpu.VMEM((R, cr + 8, width), F32),
        pltpu.VMEM((R, cr + 8, width), F32),
        pltpu.VMEM((n, cr, width), F32),
        pltpu.VMEM((R, n, cr, width), F32),
        dma((8,)),
    ] + [dma((half, T))] * 4 + [dma((R, T))] * 4 + [dma((half, T))] * 4 + [
        dma((n,)), dma((n,)), dma((R,)), dma((R,)), dma((n,)), dma((n,)), dma((R,)), dma((R,)),
    ]
    act, fgrad, wgrad, bgrad = pl.pallas_call(
        functools.partial(kernel, n, R, T, S),
        out_shape=(
            jax.ShapeDtypeStruct((own_rows, width), BF16),
            jax.ShapeDtypeStruct((own_rows, width), BF16),
            jax.ShapeDtypeStruct(weight.shape, F32),
            jax.ShapeDtypeStruct((1, width), F32),
        ),
        in_specs=[hbm] * 8,
        out_specs=(vmem, vmem, vmem, vmem),
        scratch_shapes=scratch,
        compiler_params=pltpu.CompilerParams(
            collective_id=0, has_side_effects=True, vmem_limit_bytes=VMEM_LIMIT),
        name="graph_layer",
    )(features.reshape(block), tiles[0], tile_rows, tile_cols, counts, weight,
      bias.reshape(1, -1), cotangent)
    results = pl.pallas_call(
        emit,
        out_shape=tuple(jax.ShapeDtypeStruct(x.shape, x.dtype)
                        for x in (act, fgrad, wgrad, bgrad)),
        in_specs=[vmem] * 4,
        out_specs=(vmem,) * 4,
        name="emit_results",
    )(act, fgrad, wgrad, bgrad)
    return results[0], results[1], results[2], results[3][0]


def solution(mesh):
    in_specs = (
        P(("blk", "rep"), None),
        P("blk", "rep", None, None),
        P("blk", "rep"),
        P("blk", "rep"),
        P("blk", "rep"),
        P(),
        P(),
        P(("blk", "rep"), None),
    )
    out_specs = (P(("blk", "rep"), None), P(("blk", "rep"), None), P(), P())
    body = functools.partial(per_device, mesh.shape["blk"], mesh.shape["rep"])
    return jax.shard_map(body, mesh=mesh, in_specs=in_specs, out_specs=out_specs, check_vma=False)
```

```python
import functools

import jax
import jax.numpy as jnp
from jax import lax
from jax.experimental import pallas as pl
from jax.experimental.pallas import tpu as pltpu
from jax.sharding import PartitionSpec as P

MESH = pl.DeviceIdType.MESH
F32 = jnp.float32
BF16 = jnp.bfloat16
VMEM_LIMIT = 63 * 1024 * 1024


def flip(index, bits):
    out = index
    bit = 1
    while bit <= bits:
        if bits & bit:
            out = out + bit - 2 * bit * ((index // bit) % 2)
        bit *= 2
    return out


def kernel(n, R, T, S, features, tiles, rows_in, cols_in, counts_in, weight, bias_in, cotangent,
           act_out, fgrad_out, wgrad_out, bgrad_out,
           rows, cols, counts, bias, feat, tile_v, weight_v, cot_v, prod, total_v, send_b, recv_b, grads,
           send_d1, recv_d1, send_d2, recv_d2,
           send_w1, recv_w1, send_w2, recv_w2, slab_w3, slab_w4,
           load_sem, az_send, az_recv, ay_send, ay_recv, b_send, b_recv, c_send, c_recv,
           d1_send, d1_recv, d2_send, d2_recv, w1_send, w1_recv, w2_send, w2_recv,
           w3_send, w3_recv, w4_send, w4_recv):
    b = lax.axis_index("blk")
    r = lax.axis_index("rep")
    half = n // 2
    size = tiles.shape[1]
    width = weight.shape[1]
    fb = weight.shape[0] // n
    fr = fb // R
    cb = send_w1.shape[1] - 16
    cr = send_w2.shape[1] - 8
    partner = flip(b, 1)

    def remote(src, dst, ssem, rsem, device):
        return pltpu.make_async_remote_copy(
            src_ref=src, dst_ref=dst, send_sem=ssem, recv_sem=rsem,
            device_id=device, device_id_type=MESH)

    loads = [
        pltpu.make_async_copy(features, feat.at[pl.ds(b * T, T)], load_sem.at[0]),
        pltpu.make_async_copy(tiles, tile_v, load_sem.at[1]),
        pltpu.make_async_copy(weight, weight_v, load_sem.at[2]),
        pltpu.make_async_copy(cotangent, cot_v, load_sem.at[3]),
        pltpu.make_async_copy(rows_in, rows, load_sem.at[4]),
        pltpu.make_async_copy(cols_in, cols, load_sem.at[5]),
        pltpu.make_async_copy(counts_in, counts, load_sem.at[6]),
        pltpu.make_async_copy(bias_in, bias, load_sem.at[7]),
    ]
    for c in loads:
        c.start()

    barrier = pltpu.get_barrier_semaphore()
    for s in range(1, n):
        pl.semaphore_signal(barrier, inc=1, device_id=(flip(b, s), r), device_id_type=MESH)
    for s in range(1, R):
        pl.semaphore_signal(barrier, inc=1, device_id=(b, flip(r, s)), device_id_type=MESH)
    pl.semaphore_wait(barrier, n - 1 + R - 1)

    loads[0].wait()
    order = sorted(range(1, half), key=lambda q: (q.bit_count(), q))
    own = [feat.at[b * T + t] for t in range(T)]
    az, ay = {}, {}
    for t in range(T):
        ay[0, t] = remote(own[t], own[t], ay_send.at[0, t], ay_recv.at[0, t], (partner, r))
        ay[0, t].start()
    for q in order:
        for t in range(T):
            az[q, t] = remote(own[t], own[t], az_send.at[q, t], az_recv.at[q, t],
                              (flip(b, 2 * q), r))
            az[q, t].start()
    for q in order:
        for t in range(T):
            az[q, t].wait_recv()
            tile = feat.at[flip(b, 2 * q) * T + t]
            ay[q, t] = remote(tile, tile, ay_send.at[q, t], ay_recv.at[q, t], (partner, r))
            ay[q, t].start()
    for c in loads[1:]:
        c.wait()
    for q in [0] + order:
        for t in range(T):
            ay[q, t].wait_recv()

    live = [lax.convert_element_type(k < counts[0, 0], F32) for k in range(S)]
    row_of = [rows[0, k] for k in range(S)]
    col_of = [cols[0, k] for k in range(S)]

    for k in range(S):
        prod[k] = jnp.dot(tile_v[k], feat[col_of[k]], preferred_element_type=F32)

    step = 32

    def combine(index_of, target, dest):
        w = [jnp.where(index_of[k] == target, live[k], 0.0) for k in range(S)]

        def chunk(i, carry):
            at = pl.multiple_of(i * step, step)
            total = prod[0, pl.ds(at, step), :] * w[0]
            for k in range(1, S):
                total = total + prod[k, pl.ds(at, step), :] * w[k]
            dest(at, total)
            return carry

        lax.fori_loop(0, size // step, chunk, 0)

    bs, cs = {}, {}
    peers = sorted(range(1, R), key=lambda s: (-(s // 2), s))
    for t in range(T):
        for s in peers:
            peer = flip(r, s)

            def put(at, value, t=t, s=s):
                send_b[s, t, pl.ds(at, step), :] = value.astype(BF16)

            combine(row_of, peer * T + t, put)
            bs[s, t] = remote(send_b.at[s, t], recv_b.at[s, t], b_send.at[s, t],
                              b_recv.at[s, t], (b, peer))
            bs[s, t].start()
    for t in range(T):

        def put(at, value, t=t):
            total_v[t, pl.ds(at, step), :] = value

        combine(row_of, r * T + t, put)
    agg_parts, act_parts = [], []
    for t in range(T):
        total = total_v[t]
        for s in peers[::-1]:
            bs[s, t].wait_recv()
            total = total + recv_b[s, t].astype(F32)
        agg_t = total.astype(BF16)
        pre = jnp.dot(agg_t, weight_v[...], preferred_element_type=F32) + bias[...]
        sig = jax.nn.sigmoid(pre)
        cot_t = cot_v[t * size:(t + 1) * size, :].astype(F32)
        act_t = (cot_t * sig * (1.0 + pre * (1.0 - sig))).astype(BF16)
        grads[r * T + t] = lax.dot_general(
            act_t, weight_v[...], (((1,), (1,)), ((), ())),
            preferred_element_type=F32).astype(BF16)
        here = grads.at[r * T + t]
        for s in [s for s in peers if s % 2 == 0] + [1]:
            cs[s, t] = remote(here, here, c_send.at[s, t], c_recv.at[s, t], (b, flip(r, s)))
            cs[s, t].start()
        act_out[t * size:(t + 1) * size, :] = (pre * sig).astype(BF16)
        agg_parts.append(agg_t)
        act_parts.append(act_t)
    agg = jnp.concatenate(agg_parts, axis=0)
    act_grad = jnp.concatenate(act_parts, axis=0)

    part = lax.dot_general(agg, act_grad, (((0,), (0,)), ((), ())), preferred_element_type=F32)
    bias_part = jnp.sum(act_grad.astype(F32).reshape(-1, 16, width), axis=0).astype(BF16)
    part = part.astype(BF16)
    for q in range(n):
        send_w1[q, :fb, :] = part[q * fb:(q + 1) * fb, :]
        send_w1[q, cb:, :] = bias_part
    w1 = {}
    for s in range(1, n):
        peer = flip(b, s)
        w1[s] = remote(send_w1.at[peer], recv_w1.at[b], w1_send.at[s], w1_recv.at[s], (peer, r))
        w1[s].start()
    recv_w1[b] = send_w1[b]

    for t in range(T):
        for s in peers:
            if s % 2 == 0:
                cs[s, t].wait_recv()
                block = grads.at[flip(r, s) * T + t]
                cs[s + 1, t] = remote(block, block, c_send.at[s + 1, t], c_recv.at[s + 1, t],
                                      (b, flip(r, 1)))
                cs[s + 1, t].start()
    for t in range(T):
        for s in peers:
            if s % 2 == 1:
                cs[s, t].wait_recv()
    for k in range(S):
        prod[k] = lax.dot_general(tile_v[k], grads[row_of[k]], (((0,), (0,)), ((), ())),
                                  preferred_element_type=F32)

    far = order
    d1, d2, w2, w3, w4 = {}, {}, {}, {}, {}

    def to_partner(q):
        goal = flip(partner, 2 * q)
        for t in range(T):
            def put(at, value, t=t, q=q):
                send_d1[q, t, pl.ds(at, step), :] = value.astype(BF16)
            combine(col_of, goal * T + t, put)
            d1[q, t] = remote(send_d1.at[q, t], recv_d1.at[q, t], d1_send.at[q, t],
                              d1_recv.at[q, t], (partner, r))
            d1[q, t].start()

    def to_owner(q):
        goal = flip(b, 2 * q)
        for t in range(T):
            def put(at, value, t=t, q=q):
                other = recv_d1[q, t, pl.ds(at, step), :].astype(F32)
                send_d2[q, t, pl.ds(at, step), :] = (value + other).astype(BF16)
            d1[q, t].wait_recv()
            combine(col_of, goal * T + t, put)
            d2[q, t] = remote(send_d2.at[q, t], recv_d2.at[q, t], d2_send.at[q, t],
                              d2_recv.at[q, t], (goal, r))
            d2[q, t].start()

    def weights_over_rep():
        for s in range(1, n):
            w1[s].wait_recv()
        total = recv_w1[0].astype(F32)
        for q in range(1, n):
            total = total + recv_w1[q].astype(F32)
        biases = total[cb:cb + 8, :] + total[cb + 8:, :]
        for j in range(R):
            send_w2[j, :fr, :] = total[j * fr:(j + 1) * fr, :]
            send_w2[j, cr:, :] = biases
        for s in peers:
            peer = flip(r, s)
            w2[s] = remote(send_w2.at[peer], recv_w2.at[r], w2_send.at[s], w2_recv.at[s],
                           (b, peer))
            w2[s].start()
        recv_w2[r] = send_w2[r]

    scale = 1.0 / (n * R)

    def weights_back():
        for s in peers:
            w2[s].wait_recv()
        total = recv_w2[0]
        for j in range(1, R):
            total = total + recv_w2[j]
        bgrad_out[...] = jnp.sum(total[cr:, :], axis=0, keepdims=True) * scale
        slab_w3[b] = total[:cr, :] * scale
        for s in range(1, n):
            w3[s] = remote(slab_w3.at[b], slab_w3.at[b], w3_send.at[s], w3_recv.at[s],
                           (flip(b, s), r))
            w3[s].start()

    to_partner(far[0])
    weights_over_rep()
    for q in far[1:]:
        to_partner(q)
    weights_back()
    to_partner(0)
    for q in far:
        to_owner(q)

    for s in range(1, n):
        w3[s].wait_recv()
    for s in peers:
        w4[s] = remote(slab_w3, slab_w4.at[r], w4_send.at[s], w4_recv.at[s], (b, flip(r, s)))
        w4[s].start()
    slab_w4[r] = slab_w3[...]

    for t in range(T):
        d1[0, t].wait_recv()
        for q in far:
            d2[q, t].wait_recv()

        def put(at, value, t=t):
            value = value + recv_d1[0, t, pl.ds(at, step), :].astype(F32)
            for q in far:
                value = value + recv_d2[q, t, pl.ds(at, step), :].astype(F32)
            fgrad_out[pl.ds(t * size + at, step), :] = value.astype(BF16)
        combine(col_of, b * T + t, put)

    for s in peers:
        w4[s].wait_recv()
    for j in range(n):
        for q in range(R):
            wgrad_out[j * fb + q * fr:j * fb + (q + 1) * fr, :] = slab_w4[q, j, :fr, :]

    for group in (az.values(), ay.values(), bs.values(), cs.values(), d1.values(), d2.values(),
                  w1.values(), w2.values(), w3.values(), w4.values()):
        for c in group:
            c.wait_send()


def emit(a, f, w, g, a_out, f_out, w_out, g_out):
    a_out[...] = a[...]
    f_out[...] = f[...]
    w_out[...] = w[...]
    g_out[...] = g[...]


def per_device(n, R, features, tiles, tile_rows, tile_cols, counts, weight, bias, cotangent):
    own_rows, width = features.shape
    S, size = tiles.shape[1], tiles.shape[2]
    T = own_rows // size
    half = n // 2
    fb = weight.shape[0] // n
    fr = fb // R
    cb, cr = max(16, fb), max(8, fr)
    hbm = pl.BlockSpec(memory_space=pltpu.HBM)
    vmem = pl.BlockSpec(memory_space=pltpu.VMEM)
    block = (T, size, width)
    dma = pltpu.SemaphoreType.DMA
    scratch = [
        pltpu.SMEM(tile_rows.shape, jnp.int32),
        pltpu.SMEM(tile_cols.shape, jnp.int32),
        pltpu.SMEM(counts.shape, jnp.int32),
        pltpu.VMEM((1, width), F32),
        pltpu.VMEM((n * T, size, width), BF16),
        pltpu.VMEM((S, size, size), BF16),
        pltpu.VMEM(weight.shape, BF16),
        pltpu.VMEM((own_rows, width), BF16),
        pltpu.VMEM((S, size, width), F32),
        pltpu.VMEM(block, F32),
        pltpu.VMEM((R,) + block, BF16),
        pltpu.VMEM((R,) + block, BF16),
        pltpu.VMEM((R * T, size, width), BF16),
    ] + [pltpu.VMEM((half,) + block, BF16)] * 4 + [
        pltpu.VMEM((n, cb + 16, width), BF16),
        pltpu.VMEM((n, cb + 16, width), BF16),
        pltpu.VMEM((R, cr + 8, width), F32),
        pltpu.VMEM((R, cr + 8, width), F32),
        pltpu.VMEM((n, cr, width), F32),
        pltpu.VMEM((R, n, cr, width), F32),
        dma((8,)),
    ] + [dma((half, T))] * 4 + [dma((R, T))] * 4 + [dma((half, T))] * 4 + [
        dma((n,)), dma((n,)), dma((R,)), dma((R,)), dma((n,)), dma((n,)), dma((R,)), dma((R,)),
    ]
    act, fgrad, wgrad, bgrad = pl.pallas_call(
        functools.partial(kernel, n, R, T, S),
        out_shape=(
            jax.ShapeDtypeStruct((own_rows, width), BF16),
            jax.ShapeDtypeStruct((own_rows, width), BF16),
            jax.ShapeDtypeStruct(weight.shape, F32),
            jax.ShapeDtypeStruct((1, width), F32),
        ),
        in_specs=[hbm] * 8,
        out_specs=(vmem, vmem, vmem, vmem),
        scratch_shapes=scratch,
        compiler_params=pltpu.CompilerParams(
            collective_id=0, has_side_effects=True, vmem_limit_bytes=VMEM_LIMIT),
        name="graph_layer",
    )(features.reshape(block), tiles[0], tile_rows, tile_cols, counts, weight,
      bias.reshape(1, -1), cotangent)
    results = pl.pallas_call(
        emit,
        out_shape=tuple(jax.ShapeDtypeStruct(x.shape, x.dtype)
                        for x in (act, fgrad, wgrad, bgrad)),
        in_specs=[vmem] * 4,
        out_specs=(vmem,) * 4,
        name="emit_results",
    )(act, fgrad, wgrad, bgrad)
    return results[0], results[1], results[2], results[3][0]


def solution(mesh):
    in_specs = (
        P(("blk", "rep"), None),
        P("blk", "rep", None, None),
        P("blk", "rep"),
        P("blk", "rep"),
        P("blk", "rep"),
        P(),
        P(),
        P(("blk", "rep"), None),
    )
    out_specs = (P(("blk", "rep"), None), P(("blk", "rep"), None), P(), P())
    body = functools.partial(per_device, mesh.shape["blk"], mesh.shape["rep"])
    return jax.shard_map(body, mesh=mesh, in_specs=in_specs, out_specs=out_specs, check_vma=False)
```
